256 devices in a mesh: seq: 32 (over y_hi, z, core), mp: 8 (over y_lo, x).
Axes of the slice: x: 4, y: 4 (y_hi: 2, y_lo: 2; y = y_hi * 2 + y_lo), z: 8, core: 2. Of those that a mesh axis runs over, the one named last changes fastest.
Arguments:
- tokens: bfloat16 [8192, 4096], P('seq', 'mp'), may hold values from -16 to 16
- grad_out: bfloat16 [8192, 4096], P('seq', 'mp'), may hold values from -6 to 6
- w_query: bfloat16 [4096, 4096], P('seq', 'mp'), may hold values from -0.09375 to 0.09375
- w_key: bfloat16 [4096, 1024], P('seq', 'mp'), may hold values from -0.09375 to 0.09375
- w_value: bfloat16 [4096, 1024], P('seq', 'mp'), may hold values from -0.09375 to 0.09375
- doc_lengths: int32 [4], replicated, may hold values from 1 to 48, 64 in all
Outputs:
- grad_tokens: bfloat16 [8192, 4096], P('seq', 'mp')
- grad_w_query: float32 [4096, 4096], P('seq', 'mp')
- grad_w_key: float32 [4096, 1024], P('seq', 'mp')
- grad_w_value: float32 [4096, 1024], P('seq', 'mp')
The draws below stay inside these ranges and needn't reach their ends.
Inputs may be any that keep to these rules, and one draw needn't show every extreme that they name: `doc_lengths`: the lengths sum to 64.
All inputs are finite; a program needn't handle non-finite values.
Results may differ from the reference program's by a relative error of at most 0.03.
The reference program's roundings to bfloat16 on the way (of `query`, `probs_low` and `grad_scores`) count: a program that leaves them out, or rounds other values in their place, can miss the bound.
Values may be sent and summed in bfloat16 or wider, within the bound.
No kernel may reach another device: no remote copies, remote signals or barrier semaphores. Data moves between devices by JAX's collectives and lax.ppermute only.
A program may use at most 64 MiB of HBM per device.

```python
import math
import jax
import jax.numpy as jnp
import numpy as np
from jax import lax

D = 4096
HEADS = 32
KV_HEADS = 8
HEAD_DIM = 128
WINDOW = 4096
TOK_DEV = 256
ALIGN = 128
DOCS = 4
LIST = 8192
KV_DIM = 1024
TOTAL_BLOCKS = 64
MOST_BLOCKS = 48
N_SEQ = 32


def draw_tokens(key, part):
    first_key = jax.random.fold_in(key, 0)
    base = jax.random.normal(first_key, (LIST, D), jnp.float32)
    values = base
    return jnp.clip(values, -16.0, 16.0).astype(jnp.bfloat16)


def steps_of(stream_key, dims, cuts, smallest, top_value):
    loudness = 1.0
    for dim, blocks in cuts:
        draws = jax.random.uniform(jax.random.fold_in(jax.random.fold_in(stream_key, 6), dim), (blocks,), jnp.float32, smallest / len(cuts), top_value / len(cuts))
        loudness = loudness * jnp.repeat(jnp.exp(draws), dims[dim] // blocks).reshape((-1,) + (1,) * (len(dims) - 1 - dim))
    return loudness


def split_up(number_of, total, bound, slope):
    portions = [(1 << 20) // math.isqrt(grade ** slope) + 1 for grade in range(2, number_of + 1)]
    rest, given = total - bound - (number_of - 1), [1] * (number_of - 1)
    while rest > 0:
        free = [i for i in range(number_of - 1) if given[i] < bound]
        pool, remaining = sum([portions[i] for i in free]), rest
        for i in free:
            extra = min(bound - given[i], max(1, remaining * portions[i] // pool), rest)
            given[i] = given[i] + extra
            rest = rest - extra
    return np.array([bound] + given)


def uneven_parts(own_key, amount, total, most, skew):
    if amount == 2:
        one = jax.random.randint(own_key, (), max(1, total - most), min(most, total - 1) + 1)
        return jnp.stack([one, total - one])
    sizes = jnp.asarray(split_up(amount, total, most, skew), jnp.int32)
    pairs = (amount - 1) // 2
    donor, taker = sizes[1:1 + 2 * pairs:2], sizes[2:2 + 2 * pairs:2]
    slack = jnp.minimum(donor - 1, most - taker)
    passed = jax.random.randint(jax.random.fold_in(own_key, 1), (pairs,), 0, 1 << 20) % (slack + 1)
    sizes = sizes.at[1:1 + 2 * pairs:2].set(donor - passed).at[2:2 + 2 * pairs:2].set(taker + passed)
    return sizes[jax.random.permutation(jax.random.fold_in(own_key, 2), amount)]


def centred(stream_key, dims, deviation, limit, shards=(), kind=jnp.bfloat16):
    array = jax.random.normal(stream_key, dims, jnp.float32) * deviation
    if len(shards) > 0:
        array = steps_of(stream_key, dims, shards, -0.22, 0.18) * array
    return jnp.clip(array, min=-limit, max=limit).astype(kind)


def setup_inputs(seed: int = 0) -> dict:
    splits = jax.random.split(jax.random.key(seed), 7)
    tokens = draw_tokens(jax.random.fold_in(splits[6], 71), 0)
    grad_out = centred(splits[1], (LIST, D), 1.0, 6.0, ((0, 32), (1, 8)))
    w_query = centred(splits[2], (D, D), D ** -0.5, 0.09375, ((0, 32), (1, 8)))
    w_key = centred(splits[3], (D, KV_DIM), D ** -0.5, 0.09375, ((0, 32), (1, 8)))
    w_value = centred(splits[4], (D, KV_DIM), D ** -0.5, 0.09375, ((0, 32), (1, 8)))
    doc_lengths = uneven_parts(splits[5], DOCS, TOTAL_BLOCKS, MOST_BLOCKS, 2).astype(jnp.int32)
    return dict(tokens=tokens, grad_out=grad_out, w_query=w_query, w_key=w_key, w_value=w_value, doc_lengths=doc_lengths)


THETA = 10000.0


def list_offsets(positions, ends, lengths):
    after = positions[:, None] >= ends[None, :]
    member = jnp.sum(after.astype(jnp.int32), axis=1).astype(jnp.int32)
    before = jnp.sum(jnp.where(after, lengths[None, :] * ALIGN, 0), axis=1).astype(jnp.int32)
    return member, (positions - before).astype(jnp.int32)


def rope_tables(offsets):
    half = HEAD_DIM // 2
    inverse = THETA ** (-(jnp.arange(half, dtype=jnp.float32) * 2.0 / HEAD_DIM))
    angle = offsets.astype(jnp.float32)[:, None] * inverse[None, :]
    angle = jnp.concatenate([angle, angle], axis=1)
    return jnp.cos(angle), jnp.sin(angle)


def rotate(vectors, cosine, sine, direction):
    half = vectors.shape[-1] // 2
    turned = jnp.concatenate([-vectors[..., half:], vectors[..., :half]], axis=-1)
    return vectors * cosine[:, None, :] + direction * turned * sine[:, None, :]


def reference(tokens, grad_out, w_query, w_key, w_value, doc_lengths):
    group = HEADS // KV_HEADS
    scale = HEAD_DIM ** -0.5
    ends = (jnp.cumsum(doc_lengths) * ALIGN).astype(jnp.int32)
    positions = jnp.arange(LIST, dtype=jnp.int32)
    member, offsets = list_offsets(positions, ends, doc_lengths)
    cosine, sine = rope_tables(offsets)
    query = rotate(jnp.dot(tokens, w_query, preferred_element_type=jnp.float32).reshape(LIST, HEADS, HEAD_DIM), cosine, sine, 1.0)
    query = query.astype(jnp.bfloat16).reshape(LIST, KV_HEADS, group, HEAD_DIM)
    keys = rotate(jnp.dot(tokens, w_key, preferred_element_type=jnp.float32).reshape(LIST, KV_HEADS, HEAD_DIM), cosine, sine, 1.0)
    keys = keys.astype(jnp.bfloat16)
    values = jnp.dot(tokens, w_value, preferred_element_type=jnp.float32).astype(jnp.bfloat16).reshape(LIST, KV_HEADS, HEAD_DIM)
    grad_heads = grad_out.reshape(LIST, KV_HEADS, group, HEAD_DIM)
    front = jnp.zeros((WINDOW, KV_HEADS, HEAD_DIM), jnp.bfloat16)
    keys_pad = jnp.concatenate([front, keys], axis=0)
    values_pad = jnp.concatenate([front, values], axis=0)
    member_pad = jnp.concatenate([-jnp.ones((WINDOW,), jnp.int32), member], axis=0)
    reach = WINDOW + TOK_DEV

    def one_block(carry, index):
        key_acc, value_acc = carry
        start = (index * TOK_DEV).astype(jnp.int32)
        query_block = lax.dynamic_slice_in_dim(query, start, TOK_DEV, 0).astype(jnp.float32)
        grad_block = lax.dynamic_slice_in_dim(grad_heads, start, TOK_DEV, 0).astype(jnp.float32)
        key_block = lax.dynamic_slice_in_dim(keys_pad, start, reach, 0).astype(jnp.float32)
        value_block = lax.dynamic_slice_in_dim(values_pad, start, reach, 0).astype(jnp.float32)
        query_pos = start + jnp.arange(TOK_DEV, dtype=jnp.int32)
        key_pos = start - WINDOW + jnp.arange(reach, dtype=jnp.int32)
        query_member = lax.dynamic_slice_in_dim(member, start, TOK_DEV, 0)
        key_member = lax.dynamic_slice_in_dim(member_pad, start, reach, 0)
        gap = query_pos[:, None] - key_pos[None, :]
        live = (gap >= 0) & (gap < WINDOW) & (query_member[:, None] == key_member[None, :])
        scores = jnp.einsum("qagd,kad->agqk", query_block, key_block) * scale
        scores = jnp.where(live, scores, -jnp.inf)
        top = jnp.max(scores, axis=-1, keepdims=True)
        weights = jnp.exp(scores - top)
        probs = weights / jnp.sum(weights, axis=-1, keepdims=True)
        probs_low = lax.optimization_barrier(probs.astype(jnp.bfloat16)).astype(jnp.float32)
        attended = jnp.einsum("agqk,kad->qagd", probs_low, value_block)
        delta = jnp.sum(grad_block * attended, axis=-1)
        grad_probs = jnp.einsum("qagd,kad->agqk", grad_block, value_block)
        grad_scores = probs * (grad_probs - jnp.transpose(delta, (1, 2, 0))[..., None])
        grad_scores = lax.optimization_barrier(grad_scores.astype(jnp.bfloat16)).astype(jnp.float32)
        grad_query = scale * jnp.einsum("agqk,kad->qagd", grad_scores, key_block)
        grad_keys = scale * jnp.einsum("agqk,qagd->kad", grad_scores, query_block)
        grad_values = jnp.einsum("agqk,qagd->kad", probs_low, grad_block)
        key_acc = lax.dynamic_update_slice_in_dim(key_acc, lax.dynamic_slice_in_dim(key_acc, start, reach, 0) + grad_keys, start, 0)
        value_acc = lax.dynamic_update_slice_in_dim(value_acc, lax.dynamic_slice_in_dim(value_acc, start, reach, 0) + grad_values, start, 0)
        return (key_acc, value_acc), grad_query

    empty = jnp.zeros((LIST + WINDOW, KV_HEADS, HEAD_DIM), jnp.float32)
    (key_acc, value_acc), query_grads = lax.scan(one_block, (empty, empty), jnp.arange(LIST // TOK_DEV, dtype=jnp.int32))
    dquery = query_grads.reshape(LIST, HEADS, HEAD_DIM)
    grad_query = rotate(dquery, cosine, sine, -1.0).astype(jnp.bfloat16).reshape(LIST, D)
    grad_key = rotate(key_acc[WINDOW:], cosine, sine, -1.0).astype(jnp.bfloat16).reshape(LIST, KV_DIM)
    grad_value = value_acc[WINDOW:].astype(jnp.bfloat16).reshape(LIST, KV_DIM)
    grad_all = jnp.concatenate([grad_query, grad_key, grad_value], axis=1)
    weights_all = jnp.concatenate([w_query, w_key, w_value], axis=1)
    grad_tokens = lax.dot_general(grad_all, weights_all, (((1,), (1,)), ((), ())), preferred_element_type=jnp.float32).astype(jnp.bfloat16)

    def weight_block(total, index):
        start = (index * TOK_DEV).astype(jnp.int32)
        rows_block = lax.dynamic_slice_in_dim(tokens, start, TOK_DEV, 0)
        grads_block = lax.dynamic_slice_in_dim(grad_all, start, TOK_DEV, 0)
        part = lax.dot_general(rows_block, grads_block, (((0,), (0,)), ((), ())), preferred_element_type=jnp.float32)
        part = lax.optimization_barrier(part.astype(jnp.bfloat16))
        return total + part.astype(jnp.float32), None

    total, _ = lax.scan(weight_block, jnp.zeros((D, D + 2 * KV_DIM), jnp.float32), jnp.arange(N_SEQ, dtype=jnp.int32))
    return (grad_tokens, total[:, :D], total[:, D:D + KV_DIM], total[:, D + KV_DIM:])
```

```python
import functools
import math

import jax
import jax.numpy as jnp
from jax import lax
from jax.experimental import pallas as pl
from jax.experimental.pallas import tpu as pltpu
from jax.sharding import Mesh, PartitionSpec as P

HEAD_DIM = 128
WINDOW = 4096
ALIGN = 128
THETA = 10000.0
ROWS = 256
HEADS = 4
CHUNKS = WINDOW // ROWS + 1
DOCS = 4
SCALE = HEAD_DIM**-0.5
LOG2E = 1.0 / math.log(2.0)
NY, NZ, NC, NL, NX = 2, 8, 2, 2, 4
BF = jnp.bfloat16
F32 = jnp.float32
ANY = pl.BlockSpec(memory_space=pl.ANY)
VM = pl.BlockSpec(memory_space=pltpu.VMEM)
SM = pl.BlockSpec(memory_space=pltpu.SMEM)
LIMIT = 62 * 1024 * 1024


def turned(value, axis, by):
    n = lax.axis_size(axis)
    return lax.ppermute(value, axis, [(i, (i + by) % n) for i in range(n)])


def from_mp(value, ry, rx):
    pairs = []
    for dst in range(NL * NX):
        src = ((dst // NX + ry) % NL) * NX + (dst % NX + rx) % NX
        pairs.append((src, dst))
    return lax.ppermute(value, "mp", pairs)


def to_mp(value, ry, rx):
    pairs = []
    for src in range(NL * NX):
        dst = ((src // NX + ry) % NL) * NX + (src % NX + rx) % NX
        pairs.append((src, dst))
    return lax.ppermute(value, "mp", pairs)


def ring_gather(value):
    half = value.shape[0] // 2
    got = {0: [value]}
    up, down = value, value
    for d in range(1, 4):
        up, down = turned(up, "z", 1), turned(down, "z", -1)
        got[NZ - d], got[d] = [up], [down]
    got[4] = [turned(up[:half], "z", 1), turned(down[half:], "z", -1)]
    return [got[r] for r in range(NZ)]


def added(a, b):
    return (a.astype(F32) + b.astype(F32)).astype(BF)


def ring_scatter(terms):
    half = terms[4].shape[1] // 2
    up = turned(terms[4][:, :half], "z", 1)
    down = turned(terms[4][:, half:], "z", -1)
    up = jnp.concatenate([added(terms[3][:, :half], up), terms[3][:, half:]], axis=1)
    down = jnp.concatenate([terms[5][:, :half], added(terms[5][:, half:], down)], axis=1)
    for r in (2, 1, 0):
        up, down = turned(up, "z", 1), turned(down, "z", -1)
        if r:
            up, down = added(terms[r], up), added(terms[NZ - r], down)
    total = terms[0].astype(F32) + up.astype(F32) + down.astype(F32)
    other = turned(total[1].astype(BF), "yh", 1)
    return total[0] + other.astype(F32)


def load_tokens(at, tok_refs, dst, sems):
    copies = []
    for i, ref in enumerate(tok_refs):
        ry, rx = i // NX, i % NX
        m = lax.rem(at[3] + ry, NL) * NX + lax.rem(at[4] + rx, NX)
        cols = pl.ds(pl.multiple_of(m * 256, 256), 256)
        copies.append(pltpu.make_async_copy(ref, dst.at[:, cols], sems.at[i]))
    return copies


def load_panel(at, panel_refs, dst, sems):
    copies = []
    k = 0
    for ry in range(NY):
        for rz in range(NZ):
            parts = 2 if rz == 4 else 1
            y, z = lax.rem(at[0] + ry, NY), lax.rem(at[1] + rz, NZ)
            base = (y * NZ + z) * 128
            for part in range(parts):
                size = 128 // parts
                start = pl.multiple_of(base + part * size, size)
                copies.append(
                    pltpu.make_async_copy(panel_refs[k], dst.at[pl.ds(start, size)], sems.at[k])
                )
                k += 1
    return copies


N_PANEL = 2 * 9
N_TOK = 8


def project_kernel(*refs):
    at = refs[0]
    toks, panel = refs[1 : 1 + N_TOK], refs[1 + N_TOK : 1 + N_TOK + N_PANEL]
    own, other, tok_v, pan_v, sem_t, sem_p = refs[1 + N_TOK + N_PANEL :]
    copies = load_tokens(at, toks, tok_v, sem_t) + load_panel(at, panel, pan_v, sem_p)
    for copy in copies:
        copy.start()
    for copy in copies:
        copy.wait()
    n = pan_v.shape[1]
    for i, out in enumerate((own, other)):
        for j in range(n // 256):
            out[:, j * 256 : (j + 1) * 256] = jnp.dot(
                tok_v[i * ROWS : (i + 1) * ROWS, :],
                pan_v[:, j * 256 : (j + 1) * 256],
                preferred_element_type=F32,
            )


def project(at, toks, panel):
    n = panel[0].shape[1]
    part = jax.ShapeDtypeStruct((ROWS, n), F32)
    return pl.pallas_call(
        project_kernel,
        out_shape=(part, part),
        in_specs=[SM] + [ANY] * (N_TOK + N_PANEL),
        out_specs=(VM, VM),
        scratch_shapes=[
            pltpu.VMEM((2 * ROWS, 2048), BF),
            pltpu.VMEM((2048, n), BF),
            pltpu.SemaphoreType.DMA((N_TOK,)),
            pltpu.SemaphoreType.DMA((N_PANEL,)),
        ],
        cost_estimate=pl.CostEstimate(
            flops=2 * 512 * 2048 * n, bytes_accessed=2 * 2048 * (512 + n), transcendentals=0
        ),
        name="project",
    )(at, *toks, *panel)


def turn(v, cosine, sine):
    return v * cosine + pltpu.roll(v, HEAD_DIM // 2, 1) * sine


def key_kernel(mine, got, cosine, sine, out):
    total = mine[...] + got[...]
    out[:, :128] = turn(total[:, :128], cosine[...], sine[...]).astype(BF)
    out[:, 128:] = total[:, 128:].astype(BF)


def make_keys(mine, got, cosine, sine):
    return pl.pallas_call(
        key_kernel,
        out_shape=jax.ShapeDtypeStruct((ROWS, 256), BF),
        in_specs=[VM] * 4,
        out_specs=VM,
        name="make_keys",
    )(mine, got, cosine, sine)


def attend_kernel(*refs):
    at, lens, mine, got, cosine, sine, grads = refs[:7]
    own_in, par_in = refs[7:16], refs[16:25]
    gq = refs[25]
    own_out, par_out = refs[26:35], refs[35:44]
    kvs, sc, dp, qT, gT, qs, gs, acc, dqT, pl_v, ds_v, sems = refs[44:]
    core = at[2]
    seq = at[0] * (NZ * NC) + at[1] * NC + core
    copies = []
    for d in range(9):
        copies.append(pltpu.make_async_copy(own_in[d], kvs.at[17 - 2 * d], sems.at[d]))
        slot = 18 - 2 * d - 2 * core
        copies.append(pltpu.make_async_copy(par_in[d], kvs.at[slot], sems.at[9 + d]))
    for copy in copies:
        copy.start()
    first, run = [jnp.int32(0), jnp.int32(0)], jnp.int32(0)
    for k in range(DOCS - 1):
        run = run + lens[k]
        for half in range(2):
            first[half] = jnp.where(run <= 2 * seq + half, run, first[half])
    base = (seq - 16) * ROWS
    start = [f * ALIGN - base for f in first]
    lo_first = jnp.maximum(start[0], 1)
    lo_last = jnp.maximum(start[1], ROWS)
    c_lo = lax.div(lo_first, ROWS)
    c_full = jnp.minimum(lax.div(lo_last + (ROWS - 1), ROWS), CHUNKS - 1)
    c_full = jnp.maximum(c_full, c_lo)
    for h in range(HEADS):
        cols = slice(h * 128, (h + 1) * 128)
        rows = slice(h * ROWS, (h + 1) * ROWS)
        q = turn(mine[:, cols] + got[:, cols], cosine[...], sine[...]).astype(BF)
        qs[rows, :] = q
        qT[:, rows] = q.astype(F32).T.astype(BF)
        g = grads[:, cols]
        gs[rows, :] = g
        gT[:, rows] = g.astype(F32).T.astype(BF)
    zero = jnp.zeros((ROWS, 256), F32)
    acc[0] = zero
    acc[18] = zero

    @pl.loop(0, c_lo)
    def _(c):
        acc[c + 1] = zero

    for copy in copies:
        copy.wait()

    lane = lax.broadcasted_iota(jnp.int32, (1, ROWS), 1)
    low = jnp.maximum(jnp.where(lane < ALIGN, start[0], start[1]), lane + 1)
    high = lane + WINDOW

    def score(c, top, masked):
        keys, values = kvs[c + 1, :, :128], kvs[c + 1, :, 128:]
        new = []
        if masked:
            at_key = lax.broadcasted_iota(jnp.int32, (ROWS, ROWS), 0) + c * ROWS
            live = (at_key >= low) & (at_key <= high)
        for h in range(HEADS):
            cols = slice(h * ROWS, (h + 1) * ROWS)
            s = jnp.dot(keys, qT[:, cols], preferred_element_type=F32)
            if masked:
                s = jnp.where(live, s, -jnp.inf)
            sc[c, :, cols] = s
            new.append(jnp.maximum(top[h], jnp.max(s.reshape(ROWS // 8, 8, ROWS), axis=0)))
            dp[c, :, cols] = jnp.dot(values, gT[:, cols], preferred_element_type=F32)
        return tuple(new)

    top = tuple(jnp.full((8, ROWS), -jnp.inf, F32) for _ in range(HEADS))
    top = lax.fori_loop(c_lo, c_full, lambda c, t: score(c, t, True), top)
    top = lax.fori_loop(c_full, CHUNKS - 1, lambda c, t: score(c, t, False), top)
    top = score(CHUNKS - 1, top, True)
    top = [jnp.max(t, axis=0, keepdims=True) for t in top]

    def weigh(c, carry):
        new = []
        for h in range(HEADS):
            cols = slice(h * ROWS, (h + 1) * ROWS)
            mass, mix = carry[h]
            e = jnp.exp2((sc[c, :, cols] - top[h]) * (SCALE * LOG2E))
            sc[c, :, cols] = e
            mass = mass + jnp.sum(e.reshape(ROWS // 8, 8, ROWS), axis=0)
            mixed = e * dp[c, :, cols]
            mix = mix + jnp.sum(mixed.reshape(ROWS // 8, 8, ROWS), axis=0)
            new.append((mass, mix))
        return tuple(new)

    none = jnp.zeros((8, ROWS), F32)
    sums = lax.fori_loop(c_lo, CHUNKS, weigh, tuple((none, none) for _ in range(HEADS)))
    part = [1.0 / jnp.sum(mass, axis=0, keepdims=True) for mass, _ in sums]
    delta = [jnp.sum(mix, axis=0, keepdims=True) * r for (_, mix), r in zip(sums, part)]
    dqT[...] = jnp.zeros_like(dqT)

    @pl.loop(c_lo, CHUNKS)
    def _(c):
        for h in range(HEADS):
            cols = slice(h * ROWS, (h + 1) * ROWS)
            p = sc[c, :, cols] * part[h]
            pl_v[:, cols] = p.astype(BF)
            ds_v[:, cols] = (p * (dp[c, :, cols] - delta[h])).astype(BF)
        acc[c + 1, :, 128:] = jnp.dot(pl_v[...], gs[...], preferred_element_type=F32)
        acc[c + 1, :, :128] = (
            jnp.dot(ds_v[...], qs[...], preferred_element_type=F32) * SCALE
        )
        dqT[...] += lax.dot_general(
            kvs[c + 1, :, :128], ds_v[...], (((0,), (0,)), ((), ())), preferred_element_type=F32
        )

    for h in range(HEADS):
        dq = dqT[:, h * ROWS : (h + 1) * ROWS].T * SCALE
        gq[:, h * 128 : (h + 1) * 128] = turn(dq, cosine[...], -sine[...]).astype(BF)
    for d in range(9):
        own_out[d][...] = acc[17 - 2 * d]
        par_out[d][...] = acc[18 - 2 * d - 2 * core].astype(BF)


def attend(at, lens, mine, got, cosine, sine, grads, own, par):
    block = (ROWS, 256)
    wide = HEADS * ROWS
    out_shape = (
        [jax.ShapeDtypeStruct((ROWS, 512), BF)]
        + [jax.ShapeDtypeStruct(block, F32)] * 9
        + [jax.ShapeDtypeStruct(block, BF)] * 9
    )
    outs = pl.pallas_call(
        attend_kernel,
        out_shape=out_shape,
        in_specs=[SM, SM] + [VM] * 5 + [ANY] * 18,
        out_specs=[VM] * 19,
        scratch_shapes=[
            pltpu.VMEM((19, ROWS, 256), BF),
            pltpu.VMEM((CHUNKS, ROWS, wide), F32),
            pltpu.VMEM((CHUNKS, ROWS, wide), F32),
            pltpu.VMEM((128, wide), BF),
            pltpu.VMEM((128, wide), BF),
            pltpu.VMEM((wide, 128), BF),
            pltpu.VMEM((wide, 128), BF),
            pltpu.VMEM((19, ROWS, 256), F32),
            pltpu.VMEM((128, wide), F32),
            pltpu.VMEM((ROWS, wide), BF),
            pltpu.VMEM((ROWS, wide), BF),
            pltpu.SemaphoreType.DMA((18,)),
        ],
        compiler_params=pltpu.CompilerParams(vmem_limit_bytes=LIMIT),
        cost_estimate=pl.CostEstimate(
            flops=17 * 10 * 256 * 1024 * 128, bytes_accessed=6 << 20, transcendentals=0
        ),
        name="attend",
    )(at, lens, mine, got, cosine, sine, grads, *own, *par)
    return outs[0], outs[1:10], outs[10:]


def key_grad_kernel(kept, got, cosine, sine, out):
    total = kept[...] + got[...].astype(F32)
    out[:, :128] = turn(total[:, :128], cosine[...], -sine[...]).astype(BF)
    out[:, 128:] = total[:, 128:].astype(BF)


def finish_keys(kept, got, cosine, sine):
    return pl.pallas_call(
        key_grad_kernel,
        out_shape=jax.ShapeDtypeStruct((ROWS, 256), BF),
        in_specs=[VM] * 4,
        out_specs=VM,
        name="finish_keys",
    )(kept, got, cosine, sine)


def weight_kernel(*refs):
    at, g_own, g_par = refs[:3]
    toks, outs = refs[3 : 3 + N_TOK], refs[3 + N_TOK : 3 + N_TOK + NZ]
    tok_v, sem_t = refs[3 + N_TOK + NZ :]
    copies = load_tokens(at, toks, tok_v, sem_t)
    for copy in copies:
        copy.start()
    for copy in copies:
        copy.wait()
    for rz in (4, 3, 5, 2, 6, 1, 7, 0):
        for ry in range(NY):
            y, z = lax.rem(at[0] + ry, NY), lax.rem(at[1] + rz, NZ)
            cols = pl.ds(pl.multiple_of((y * NZ + z) * 128, 128), 128)
            total = None
            for i, g in enumerate((g_own, g_par)):
                term = lax.dot_general(
                    tok_v[i * ROWS : (i + 1) * ROWS, cols],
                    g[...],
                    (((0,), (0,)), ((), ())),
                    preferred_element_type=F32,
                )
                term = term.astype(BF).astype(F32)
                total = term if total is None else total + term
            outs[rz][ry] = total.astype(BF)


def weight_terms(at, g_own, g_par, toks):
    n = g_own.shape[1]
    return pl.pallas_call(
        weight_kernel,
        out_shape=[jax.ShapeDtypeStruct((NY, 128, n), BF)] * NZ,
        in_specs=[SM, VM, VM] + [ANY] * N_TOK,
        out_specs=[VM] * NZ,
        scratch_shapes=[pltpu.VMEM((2 * ROWS, 2048), BF), pltpu.SemaphoreType.DMA((N_TOK,))],
        cost_estimate=pl.CostEstimate(
            flops=2 * 512 * 2048 * n, bytes_accessed=2 * 2048 * (512 + n), transcendentals=0
        ),
        name="weight_terms",
    )(at, g_own, g_par, *toks)


def token_kernel(*refs):
    at, gq_own, gq_par, gk_own, gk_par = refs[:5]
    pan_q, pan_k = refs[5 : 5 + N_PANEL], refs[5 + N_PANEL : 5 + 2 * N_PANEL]
    outs = refs[5 + 2 * N_PANEL : 5 + 2 * N_PANEL + N_TOK]
    pq_v, pk_v, sem_q, sem_k = refs[5 + 2 * N_PANEL + N_TOK :]
    copies = load_panel(at, pan_q, pq_v, sem_q) + load_panel(at, pan_k, pk_v, sem_k)
    for copy in copies:
        copy.start()
    for copy in copies:
        copy.wait()
    dims = (((1,), (1,)), ((), ()))
    for i in range(N_TOK - 1, -1, -1):
        ry, rx = i // NX, i % NX
        m = lax.rem(at[3] + ry, NL) * NX + lax.rem(at[4] + rx, NX)
        rows = pl.ds(pl.multiple_of(m * 256, 256), 256)
        for k, (gq, gk) in enumerate(((gq_own, gk_own), (gq_par, gk_par))):
            term = lax.dot_general(gq[...], pq_v[rows, :], dims, preferred_element_type=F32)
            term += lax.dot_general(gk[...], pk_v[rows, :], dims, preferred_element_type=F32)
            outs[i][k * ROWS : (k + 1) * ROWS, :] = term.astype(BF)


def token_terms(at, gq_own, gq_par, gk_own, gk_par, pan_q, pan_k):
    return pl.pallas_call(
        token_kernel,
        out_shape=[jax.ShapeDtypeStruct((2 * ROWS, 256), BF)] * N_TOK,
        in_specs=[SM] + [VM] * 4 + [ANY] * (2 * N_PANEL),
        out_specs=[VM] * N_TOK,
        scratch_shapes=[
            pltpu.VMEM((2048, 512), BF),
            pltpu.VMEM((2048, 256), BF),
            pltpu.SemaphoreType.DMA((N_PANEL,)),
            pltpu.SemaphoreType.DMA((N_PANEL,)),
        ],
        cost_estimate=pl.CostEstimate(
            flops=2 * 512 * 2048 * 768, bytes_accessed=2 * 2048 * 1280, transcendentals=0
        ),
        name="token_terms",
    )(at, gq_own, gq_par, gk_own, gk_par, *pan_q, *pan_k)


def rope_tables(seq, lengths):
    positions = seq * ROWS + jnp.arange(ROWS, dtype=jnp.int32)
    ends = jnp.cumsum(lengths) * ALIGN
    after = positions[:, None] >= ends[None, :]
    offsets = positions - jnp.sum(jnp.where(after, lengths[None, :] * ALIGN, 0), axis=1)
    half = HEAD_DIM // 2
    inverse = THETA ** (-(jnp.arange(half, dtype=F32) * 2.0 / HEAD_DIM))
    angle = offsets.astype(F32)[:, None] * inverse[None, :]
    cosine, sine = jnp.cos(angle), jnp.sin(angle)
    return jnp.concatenate([cosine, cosine], 1), jnp.concatenate([-sine, sine], 1)


def split_parity(value, core):
    parts = value.reshape(ROWS, 2, 2, 128)
    even, odd = parts[:, :, 0].reshape(ROWS, 256), parts[:, :, 1].reshape(ROWS, 256)
    first = core == 0
    return jnp.where(first, even, odd), jnp.where(first, odd, even)


def local(tokens, grad_out, w_query, w_key, w_value, doc_lengths):
    yh, z, core, mp = (lax.axis_index(a) for a in ("yh", "z", "c", "mp"))
    seq = yh * (NZ * NC) + z * NC + core
    place = jnp.arange(5, dtype=jnp.int32)
    at = jnp.where(
        place == 0,
        yh,
        jnp.where(place == 1, z, jnp.where(place == 2, core, jnp.where(place == 3, mp // NX, mp % NX))),
    )
    cosine, sine = rope_tables(seq, doc_lengths)

    w_kv = jnp.concatenate([w_key, w_value], axis=1)
    kv_other = turned(w_kv, "yh", 1)
    q_other = turned(w_query, "yh", 1)
    panel_k = sum(ring_gather(w_kv), []) + sum(ring_gather(kv_other), [])
    kept, sent = split_parity(tokens, core)
    both = jnp.concatenate([kept, turned(sent, "c", 1)], axis=0)
    toks = [from_mp(both, i // NX, i % NX) if i else both for i in range(N_TOK)]
    panel_q = sum(ring_gather(w_query), []) + sum(ring_gather(q_other), [])

    kv_mine, kv_part = project(at, toks, panel_k)
    kv = make_keys(kv_mine, turned(kv_part, "c", 1), cosine, sine)
    far = turned(kv, "yh", 1)
    own = [kv]
    for d in range(1, NZ):
        own.append(turned(jnp.where(z + d < NZ, kv, far), "z", d))
    own.append(far)
    par = [turned(v, "c", 1) for v in own]
    q_mine, q_part = project(at, toks, panel_q)
    q_got = turned(q_part, "c", 1)

    gq, own_grads, par_grads = attend(
        at, doc_lengths, q_mine, q_got, cosine, sine, grad_out, own, par
    )

    sums = [a + turned(b, "c", 1).astype(F32) for a, b in zip(own_grads, par_grads)]
    near_sum, far_sum = sums[0], sums[8]
    for d in range(1, NZ):
        back = turned(sums[d].astype(BF), "z", -d).astype(F32)
        inside = z + d < NZ
        near_sum = near_sum + jnp.where(inside, back, 0.0)
        far_sum = far_sum + jnp.where(inside, 0.0, back)
    gq_par = turned(gq, "c", 1)
    terms_q = weight_terms(at, gq, gq_par, toks)
    grad_w_query = ring_scatter(terms_q)
    gk = finish_keys(near_sum, turned(far_sum.astype(BF), "yh", 1), cosine, sine)
    gk_par = turned(gk, "c", 1)
    grad_w_kv = ring_scatter(weight_terms(at, gk, gk_par, toks))
    terms = token_terms(at, gq, gq_par, gk, gk_par, panel_q, panel_k)
    total = terms[0].astype(F32)
    for i in range(1, N_TOK):
        total = total + to_mp(terms[i], i // NX, i % NX).astype(F32)
    total = total.astype(BF)
    mine, other = total[:ROWS], turned(total[ROWS:], "c", 1)
    first = core == 0
    even, odd = jnp.where(first, mine, other), jnp.where(first, other, mine)
    grad_tokens = jnp.stack(
        [even.reshape(ROWS, 2, 128), odd.reshape(ROWS, 2, 128)], axis=2
    ).reshape(ROWS, 512)
    return grad_tokens, grad_w_query, grad_w_kv[:, :128], grad_w_kv[:, 128:]


def solution(mesh):
    split = Mesh(mesh.devices.reshape(NY, NZ, NC, NL * NX), ("yh", "z", "c", "mp"))
    placed = P(("yh", "z", "c"), "mp")
    return jax.shard_map(
        local,
        mesh=split,
        in_specs=(placed,) * 5 + (P(),),
        out_specs=(placed,) * 4,
        check_vma=False,
    )
```
